32 devices in a mesh: groups: 2 (over y), mom: 4 (over z), tm: 4 (over x, core).
Axes of the slice: x: 2, y: 2, z: 4, core: 2. Of those that a mesh axis runs over, the one named last changes fastest.
Arguments:
- panel_start: float32 [256, 4, 64, 512], P('mom', 'groups', None, 'tm'), parts along dimension 1, may hold values from -6 to 6
- block_guess: float32 [256, 4, 64, 128], P('mom', 'groups', 'tm'), parts along dimension 1, may hold values from -6 to 6
- coupling: float32 [2], P('groups'), parts along dimension 0, may hold values from 0.3 to 0.6
- slab_owner: int32 [8], P('groups'), parts along dimension 0, may hold values from 0 to 3, each once
- expiring: int32 [2], P('groups'), parts along dimension 0, may hold values from 0 to 3
- ordering: int32 [256], replicated, may hold values from 0 to 255, each once
Outputs:
- history_out: float32 [256, 4, 64, 512], P('mom', 'groups', None, 'tm'), parts along dimension 1
The draws below stay inside these ranges and needn't reach their ends.
There are 2 independent parts, one for each index of `groups`. The reference program is written for one: setup_inputs(seed, part) draws one part's arguments, and reference() takes and returns one part's arrays. A program takes and returns all parts, laid end to end along the dimension named above; an argument that names none is the same for every part. Nothing has to cross between parts.
Inputs may be any that keep to these rules, and one draw needn't show every extreme that they name: `slab_owner`: entry s is the column block that holds history slab s; each block once. `ordering`: entry j is qx * 16 + qy for the momentum of stored row j; each momentum once.
All inputs are finite; a program needn't handle non-finite values.
Results may differ from the reference program's by a relative error of at most 0.0001.
Values sent between devices are 32-bit elements; how exact they have to be, the bound alone decides.
A program may use at most 128 MiB of HBM per device.

```python
import math
import jax
import jax.numpy as jnp
from jax import lax

LSIDE = 16
K = 256
SPIN = 2
PANEL = 64
PASSES = 2
HIST = 256
N_TM = 4


def block_levels(key, shape, cuts, smallest, largest):
    gain, own = 1.0, jax.random.fold_in(key, 6)
    for axis_at, shards_of in cuts:
        heights = jnp.exp(jax.random.uniform(jax.random.fold_in(own, axis_at), (shards_of,), jnp.float32, smallest / len(cuts), largest / len(cuts)))
        gain = gain * jnp.repeat(heights, shape[axis_at] // shards_of).reshape([-1 if axis == axis_at else 1 for axis in range(len(shape))])
    return gain


def normal_values(stream_key, extent, width, most, cuts=(), kind=jnp.bfloat16):
    values = jax.random.normal(stream_key, extent, jnp.float32) * width
    if len(cuts) > 0:
        values = block_levels(stream_key, extent, cuts, -0.22, 0.18) * values
    return jnp.clip(values, min=-most, max=most).astype(kind)


def setup_inputs(seed: int = 0, part: int = 0) -> dict:
    keys = jax.random.split(jax.random.key(seed), 7)
    part_keys = jax.random.split(jax.random.fold_in(keys[6], part), 7)
    panel_start = normal_values(part_keys[0], (K, SPIN, PANEL, 2 * HIST), 1.0, 6.0, ((0, 4), (3, 4)), jnp.float32)
    block_guess = normal_values(part_keys[1], (K, SPIN, PANEL, 2 * PANEL), 1.0, 6.0, ((0, 4), (2, 4)), jnp.float32)
    coupling = jnp.clip(jnp.exp(jax.random.uniform(part_keys[2], (1,), jnp.float32, math.log(0.3), math.log(0.6))), 0.3, 0.6)
    slab_owner = jax.random.permutation(part_keys[3], N_TM).astype(jnp.int32)
    expiring = jax.random.randint(part_keys[4], (1,), 0, N_TM).astype(jnp.int32)
    ordering = jax.random.permutation(keys[5], K).astype(jnp.int32)
    return dict(panel_start=panel_start, block_guess=block_guess, coupling=coupling, slab_owner=slab_owner, expiring=expiring, ordering=ordering)


def product(left, right):
    return jnp.dot(left, right, precision=lax.Precision.HIGHEST, preferred_element_type=jnp.float32)

def contract(pattern, left, right):
    return jnp.einsum(pattern, left, right, precision=lax.Precision.HIGHEST, preferred_element_type=jnp.float32)

def tables(ordering):
    site_index = jnp.arange(K, dtype=jnp.int32)
    site_x = site_index // LSIDE
    site_y = site_index % LSIDE
    mom_x = ordering // LSIDE
    mom_y = ordering % LSIDE
    phases = (site_x[:, None] * mom_x[None, :] + site_y[:, None] * mom_y[None, :]) % LSIDE
    angles = phases.astype(jnp.float32) * (2.0 * math.pi / LSIDE)
    mirror = (-site_x % LSIDE * LSIDE + -site_y % LSIDE).astype(jnp.int32)
    return (jnp.cos(angles) / LSIDE, jnp.sin(angles) / LSIDE, mirror)

def site_sigma(mom_re, mom_im, cos_table, sin_table, mirror, strength):
    layout = mom_re.shape
    flat_re = mom_re.reshape(K, -1)
    flat_im = mom_im.reshape(K, -1)
    site_re = (product(cos_table, flat_re) - product(sin_table, flat_im)).reshape(layout)
    site_im = (product(cos_table, flat_im) + product(sin_table, flat_re)).reshape(layout)
    other_re = site_re[:, ::-1]
    other_im = site_im[:, ::-1]
    pair_re = site_re * other_re - site_im * other_im
    pair_im = site_re * other_im + site_im * other_re
    back_re = jnp.take(other_re, mirror, axis=0)
    back_im = jnp.take(other_im, mirror, axis=0)
    sig_re = (-strength * (pair_re * back_re + pair_im * back_im)).reshape(K, -1)
    sig_im = (-strength * (pair_im * back_re - pair_re * back_im)).reshape(K, -1)
    out_re = product(cos_table.T, sig_re) + product(sin_table.T, sig_im)
    out_im = product(cos_table.T, sig_im) - product(sin_table.T, sig_re)
    return (out_re.reshape(layout), out_im.reshape(layout))

def reference(panel_start, block_guess, coupling, slab_owner, expiring, ordering):
    cos_table, sin_table, mirror = tables(ordering)
    blocks = jnp.arange(N_TM, dtype=jnp.int32)
    slab_of = lax.optimization_barrier(jnp.sum(blocks[None, :] * (slab_owner[None, :] == blocks[:, None]).astype(jnp.int32), axis=1))
    position = (slab_of - expiring[0]) % N_TM
    times = position[:, None] * PANEL + jnp.arange(PANEL, dtype=jnp.int32)[None, :]
    window = N_TM * PANEL
    weights = jnp.exp(-1.5 * (window - 1 - times).astype(jnp.float32) / window) / math.sqrt(window)
    strength = coupling[0] * coupling[0]
    step_scale = 1.0 / math.sqrt(PANEL)
    split = panel_start.reshape(K, SPIN, PANEL, N_TM, 2, PANEL)
    start_re = split[:, :, :, :, 0, :]
    start_im = split[:, :, :, :, 1, :]
    current_re, current_im = (start_re, start_im)
    conv_re = jnp.zeros((K, SPIN, PANEL, PANEL), jnp.float32)
    conv_im = jnp.zeros((K, SPIN, PANEL, PANEL), jnp.float32)
    for sweep in range(PASSES):
        sig_re, sig_im = site_sigma(current_re, current_im, cos_table, sin_table, mirror, strength)
        sig_re = sig_re * weights
        sig_im = sig_im * weights
        conv_re = -(contract('ksadu,ksbdu->ksab', sig_re, current_re) + contract('ksadu,ksbdu->ksab', sig_im, current_im))
        conv_im = -(contract('ksadu,ksbdu->ksab', sig_im, current_re) - contract('ksadu,ksbdu->ksab', sig_re, current_im))
        next_re = start_re + step_scale * (contract('ksab,ksbdu->ksadu', conv_re, current_re) - contract('ksab,ksbdu->ksadu', conv_im, current_im))
        next_im = start_im + step_scale * (contract('ksab,ksbdu->ksadu', conv_re, current_im) + contract('ksab,ksbdu->ksadu', conv_im, current_re))
        current_re, current_im = (next_re, next_im)
    guess_re = block_guess[..., :PANEL]
    guess_im = block_guess[..., PANEL:]
    block_re = guess_re + step_scale * (contract('ksab,ksbc->ksac', guess_re, conv_re) - contract('ksab,ksbc->ksac', guess_im, conv_im))
    block_im = guess_im + step_scale * (contract('ksab,ksbc->ksac', guess_re, conv_im) + contract('ksab,ksbc->ksac', guess_im, conv_re))
    history = jnp.stack([current_re, current_im], axis=4)
    block = jnp.stack([block_re, block_im], axis=3)[:, :, :, None]
    owner_expiring = jnp.sum(slab_owner * (blocks == expiring[0]).astype(jnp.int32))
    chosen = (blocks == owner_expiring)[:, None, None]
    merged = jnp.where(chosen, block, history)
    return merged.reshape(K, SPIN, PANEL, 2 * window)
```

```python
import functools
import math

import jax
import jax.numpy as jnp
from jax import lax
from jax.experimental import pallas as pl
from jax.experimental.pallas import tpu as pltpu
from jax.sharding import PartitionSpec as P

LSIDE = 16
K = LSIDE * LSIDE
PANEL = 64
PASSES = 2
SPIN = 2
LANES = 2 * PANEL
CHUNKS = 2
MESH = pl.DeviceIdType.MESH


def dot(left, right):
    return jnp.dot(left, right, precision=lax.Precision.HIGHEST, preferred_element_type=jnp.float32)


def dot_t(left, right):
    return lax.dot_general(
        left, right, (((1,), (1,)), ((), ())),
        precision=lax.Precision.HIGHEST, preferred_element_type=jnp.float32,
    )


def contract(pattern, left, right):
    return jnp.einsum(
        pattern, left, right, precision=lax.Precision.HIGHEST, preferred_element_type=jnp.float32
    )


def tables(ordering):
    site_index = jnp.arange(K, dtype=jnp.int32)
    site_x = site_index // LSIDE
    site_y = site_index % LSIDE
    mom_x = ordering // LSIDE
    mom_y = ordering % LSIDE
    phases = (site_x[:, None] * mom_x[None, :] + site_y[:, None] * mom_y[None, :]) % LSIDE
    angles = phases.astype(jnp.float32) * (2.0 * math.pi / LSIDE)
    return jnp.cos(angles) / LSIDE, jnp.sin(angles) / LSIDE


def rotated(joined):
    return jnp.concatenate([-joined[..., PANEL:], joined[..., :PANEL]], axis=-1)


def pass_kernel(
    n_mom, n_tm, last, cur, start, fwd_table, back_table, wvec,
    out, conv_out, recv, sig, ret, stk, part, gath,
    local_sem, fs, fr, rs, rr, ss, sr, gs, gr,
):
    mom, tm = lax.axis_index("mom"), lax.axis_index("tm")
    rows, local_k = cur.shape[3], cur.shape[4]
    share = local_k // n_tm
    step_scale = 1.0 / math.sqrt(PANEL)
    lane = lax.broadcasted_iota(jnp.int32, (1, LANES), 1)
    low = lane < PANEL
    sign = jnp.where(low, -1.0, 1.0).astype(jnp.float32)

    def swap(x):
        return pltpu.roll(x, PANEL, 1)

    def rot(x):
        return swap(x) * sign

    barrier = pltpu.get_barrier_semaphore()
    for o in range(1, n_mom):
        pl.semaphore_signal(barrier, inc=1, device_id={"mom": lax.rem(mom + o, n_mom)}, device_id_type=MESH)
    for o in range(1, n_tm):
        pl.semaphore_signal(barrier, inc=1, device_id={"tm": lax.rem(tm + o, n_tm)}, device_id_type=MESH)
    pl.semaphore_wait(barrier, n_mom + n_tm - 2)

    mine = pl.ds(mom * local_k, local_k)
    own_share = pl.ds(tm * share, share)

    def forward(c, o):
        peer = lax.rem(mom + o, n_mom)
        return pltpu.make_async_remote_copy(
            src_ref=cur.at[c, :, peer], dst_ref=recv.at[c, :, :, mine, :],
            send_sem=fs.at[c, o], recv_sem=fr.at[c, o],
            device_id={"mom": peer}, device_id_type=MESH)

    def forward_own(c):
        return pltpu.make_async_copy(cur.at[c, :, mom], recv.at[c, :, :, mine, :], local_sem.at[c])

    def back(c, o):
        peer = lax.rem(mom + o, n_mom)
        return pltpu.make_async_remote_copy(
            src_ref=sig.at[c, :, :, pl.ds(peer * local_k, local_k), :], dst_ref=ret.at[c, :, mom],
            send_sem=rs.at[c, o], recv_sem=rr.at[c, o],
            device_id={"mom": peer}, device_id_type=MESH)

    def back_own(c):
        return pltpu.make_async_copy(sig.at[c, :, :, mine, :], ret.at[c, :, mom], local_sem.at[CHUNKS + c])

    def scatter(c, o):
        peer = lax.rem(tm + o, n_tm)
        return pltpu.make_async_remote_copy(
            src_ref=part.at[c, pl.ds(peer * share, share)], dst_ref=gath.at[c, o],
            send_sem=ss.at[c, o], recv_sem=sr.at[c, o],
            device_id={"tm": peer}, device_id_type=MESH)

    def gather(c, o):
        peer = lax.rem(tm + o, n_tm)
        return pltpu.make_async_remote_copy(
            src_ref=conv_out.at[c, own_share], dst_ref=conv_out.at[c, own_share],
            send_sem=gs.at[c, o], recv_sem=gr.at[c, o],
            device_id={"tm": peer}, device_id_type=MESH)

    for c in range(CHUNKS):
        for o in range(1, n_mom):
            forward(c, o).start()
        forward_own(c).start()

    flat_cur = cur.reshape(CHUNKS * SPIN * n_mom * rows * local_k, LANES)
    flat_start = start.reshape(CHUNKS * SPIN * n_mom * rows * local_k, LANES)
    flat_ret = ret.reshape(CHUNKS * SPIN * n_mom * rows * local_k, LANES)
    group = n_mom * rows

    @pl.loop(0, local_k)
    def _(k):
        for s in range(SPIN):
            pieces = []
            for block in range(n_mom):
                for c in range(CHUNKS):
                    at = (((c * SPIN + s) * n_mom + block) * rows) * local_k + k
                    pieces.append(flat_cur[pl.ds(at, rows, stride=local_k), :])
            whole = jnp.concatenate(pieces, axis=0)
            stk[k, s, :PANEL, :] = whole
            stk[k, s, PANEL:, :] = rot(whole)

    for c in range(CHUNKS):
        for o in range(1, n_mom):
            forward(c, o).wait_recv()
        forward_own(c).wait()

        @pl.loop(0, rows)
        def _(i):
            both = jnp.concatenate([recv[c, 0, i], recv[c, 1, i]], axis=1)
            sums = dot(fwd_table[...], both)
            site, mirrored = [], []
            for s in range(SPIN):
                with_cos = sums[:K, s * LANES:(s + 1) * LANES]
                turned = rot(sums[K:, s * LANES:(s + 1) * LANES])
                site.append(with_cos + turned)
                mirrored.append(with_cos - turned)
            first, second = site
            flipped = swap(second)
            pair = (first * jnp.where(low, second, flipped)
                    + rot(first) * jnp.where(low, flipped, second)) * wvec[...]
            pair_rot = rot(pair)
            tops, bottoms = [], []
            for s in range(SPIN):
                other = mirrored[1 - s]
                flipped = swap(other)
                value = pair * jnp.where(low, other, flipped) - pair_rot * jnp.where(low, flipped, other)
                tops.append(value)
                bottoms.append(-rot(value))
            stacked = jnp.concatenate(
                [jnp.concatenate(tops, axis=1), jnp.concatenate(bottoms, axis=1)], axis=0)
            result = dot(back_table[...], stacked)
            for s in range(SPIN):
                sig[c, s, i] = result[:, s * LANES:(s + 1) * LANES]

        for o in range(1, n_mom):
            back(c, o).start()
        back_own(c).start()

    def convolve(c):
        for o in range(1, n_mom):
            back(c, o).wait_recv()
        back_own(c).wait()

        @pl.loop(0, local_k)
        def _(k):
            for s in range(SPIN):
                at = ((c * SPIN + s) * group) * local_k + k
                sigma = flat_ret[pl.ds(at, group, stride=local_k), :]
                part[c, k, s] = dot_t(sigma, stk[k, s])

        for o in range(1, n_tm):
            scatter(c, o).start()

    def reduce(c):
        for o in range(1, n_tm):
            scatter(c, o).wait_recv()

        @pl.loop(0, share)
        def _(k):
            for s in range(SPIN):
                total = part[c, tm * share + k, s]
                for o in range(1, n_tm):
                    total = total + gath[c, o, k, s]
                conv_out[c, tm * share + k, s] = total

        for o in range(1, n_tm):
            gather(c, o).start()

    def update(c):
        for o in range(1, n_tm):
            gather(c, o).wait_recv()

        @pl.loop(0, local_k)
        def _(k):
            for s in range(SPIN):
                at = ((c * SPIN + s) * group) * local_k + k
                base = flat_start[pl.ds(at, group, stride=local_k), :]
                new = base + step_scale * dot(conv_out[c, k, s], stk[k, s])
                if last:
                    for block in range(n_mom):
                        out[k, s, block, c] = new[block * rows:(block + 1) * rows, :]
                else:
                    flat_out = out.reshape(CHUNKS * SPIN * n_mom * rows * local_k, LANES)
                    flat_out[pl.ds(at, group, stride=local_k), :] = new

    for c in range(CHUNKS):
        convolve(c)
        if c > 0:
            reduce(c - 1)
    reduce(CHUNKS - 1)
    for c in range(CHUNKS):
        update(c)

    for c in range(CHUNKS):
        for o in range(1, n_mom):
            forward(c, o).wait_send()
            back(c, o).wait_send()
        for o in range(1, n_tm):
            scatter(c, o).wait_send()
            gather(c, o).wait_send()


def corrector(n_mom, n_tm, last, cur, start, fwd_table, back_table, wvec):
    rows, local_k = cur.shape[3], cur.shape[4]
    panel = (CHUNKS, SPIN, n_mom, rows, local_k, LANES)
    conv = (CHUNKS, local_k, SPIN, n_mom * rows, LANES)
    out_shape = (local_k, SPIN, n_mom, CHUNKS, rows, LANES) if last else panel
    dma = pltpu.SemaphoreType.DMA
    vmem = pl.BlockSpec(memory_space=pltpu.VMEM)
    return pl.pallas_call(
        functools.partial(pass_kernel, n_mom, n_tm, last),
        out_shape=(jax.ShapeDtypeStruct(out_shape, jnp.float32), jax.ShapeDtypeStruct(conv, jnp.float32)),
        in_specs=[vmem] * 5,
        out_specs=(vmem, vmem),
        scratch_shapes=[
            pltpu.VMEM((CHUNKS, SPIN, rows, K, LANES), jnp.float32),
            pltpu.VMEM((CHUNKS, SPIN, rows, K, LANES), jnp.float32),
            pltpu.VMEM(panel, jnp.float32),
            pltpu.VMEM((local_k, SPIN, LANES, LANES), jnp.float32),
            pltpu.VMEM(conv, jnp.float32),
            pltpu.VMEM((CHUNKS, n_tm, local_k // n_tm, SPIN, n_mom * rows, LANES), jnp.float32),
            dma((2 * CHUNKS,)),
            dma((CHUNKS, n_mom)), dma((CHUNKS, n_mom)),
            dma((CHUNKS, n_mom)), dma((CHUNKS, n_mom)),
            dma((CHUNKS, n_tm)), dma((CHUNKS, n_tm)),
            dma((CHUNKS, n_tm)), dma((CHUNKS, n_tm)),
        ],
        compiler_params=pltpu.CompilerParams(
            collective_id=1 if last else 0, has_side_effects=True, vmem_limit_bytes=60 * 1024 * 1024),
        name="last_pass" if last else "first_pass",
    )(cur, start, fwd_table, back_table, wvec)


def own_block(guess, conv, step_scale):
    stacked = jnp.concatenate([conv, rotated(conv)], axis=2)
    return guess + step_scale * contract("ksab,ksbc->ksac", guess, stacked)


def body(panel_start, block_guess, coupling, slab_owner, expiring, ordering):
    slab_count = lax.axis_size("tm")
    n_mom = lax.axis_size("mom")
    own_index = lax.axis_index("tm")
    cos_table, sin_table = tables(ordering)
    fwd_table = jnp.concatenate([cos_table, sin_table], axis=0)
    back_table = fwd_table.T
    back_table = jnp.concatenate([cos_table.T, sin_table.T], axis=1)
    blocks = jnp.arange(slab_count, dtype=jnp.int32)
    slab_mine = jnp.sum(blocks * (slab_owner == own_index).astype(jnp.int32))
    position = (slab_mine - expiring[0]) % slab_count
    window = slab_count * PANEL
    times = position * PANEL + jnp.arange(PANEL, dtype=jnp.int32)
    weights = jnp.exp(-1.5 * (window - 1 - times).astype(jnp.float32) / window) / math.sqrt(window)
    strength = coupling[0] * coupling[0]
    wvec = (strength * jnp.concatenate([weights, weights]))[None, :]
    step_scale = 1.0 / math.sqrt(PANEL)
    guess_full = lax.all_gather(block_guess, "tm", axis=2, tiled=True)

    local_k = panel_start.shape[0]
    rows = PANEL // (n_mom * CHUNKS)
    start = panel_start.reshape(local_k, SPIN, n_mom, CHUNKS, rows, LANES).transpose(3, 1, 2, 4, 0, 5)
    current = start
    for sweep in range(PASSES):
        current, conv = corrector(
            n_mom, slab_count, sweep == PASSES - 1, current, start, fwd_table, back_table, wvec)
    current = current.reshape(panel_start.shape)
    conv = conv.reshape(CHUNKS, local_k, SPIN, n_mom, rows, LANES).transpose(1, 2, 3, 0, 4, 5)
    block = own_block(guess_full, conv.reshape(panel_start.shape), step_scale)
    owner_expiring = jnp.sum(slab_owner * (blocks == expiring[0]).astype(jnp.int32))
    return jnp.where(own_index == owner_expiring, block, current)


def solution(mesh):
    return jax.shard_map(
        body,
        mesh=mesh,
        in_specs=(
            P("mom", "groups", None, "tm"),
            P("mom", "groups", "tm", None),
            P("groups"),
            P("groups"),
            P("groups"),
            P(),
        ),
        out_specs=P("mom", "groups", None, "tm"),
        check_vma=False,
    )
```

```python
import functools
import math

import jax
import jax.numpy as jnp
from jax import lax
from jax.experimental import pallas as pl
from jax.experimental.pallas import tpu as pltpu
from jax.sharding import PartitionSpec as P

LSIDE = 16
K = LSIDE * LSIDE
PANEL = 64
PASSES = 2
SPIN = 2
LANES = 2 * PANEL
CHUNKS = 2
MESH = pl.DeviceIdType.MESH


def tables(ordering):
    site_index = jnp.arange(K, dtype=jnp.int32)
    site_x = site_index // LSIDE
    site_y = site_index % LSIDE
    mom_x = ordering // LSIDE
    mom_y = ordering % LSIDE
    phases = (site_x[:, None] * mom_x[None, :] + site_y[:, None] * mom_y[None, :]) % LSIDE
    angles = phases.astype(jnp.float32) * (2.0 * math.pi / LSIDE)
    return jnp.cos(angles) / LSIDE, jnp.sin(angles) / LSIDE


def split(x):
    high = x.astype(jnp.bfloat16)
    return high, (x - high.astype(jnp.float32)).astype(jnp.bfloat16)


def dot3(left, right, transposed=False):
    dims = (((1,), (1 if transposed else 0,)), ((), ()))

    def one(a, b):
        return lax.dot_general(a, b, dims, preferred_element_type=jnp.float32)

    return one(left[0], right[0]) + (one(left[0], right[1]) + one(left[1], right[0]))


def step_kernel(
    n_mom, n_tm, start, guess, fwd_table, back_table, wvec, chosen,
    out, cur, recv, sig, ret, fwd_split, back_split, stk, part, conv, pair_buf, ring_buf, guess_all,
    local_sem, guess_own, fs, fr, rs, rr, ps, pr, ss, sr, gs, gr, qs, qr, ds, dr,
):
    mom, tm = lax.axis_index("mom"), lax.axis_index("tm")
    rows, local_k = cur.shape[3], cur.shape[4]
    group = n_mom * rows
    n_x = n_tm // 2
    half = local_k // 2
    share = half // n_x
    tm_x, core = tm // 2, tm % 2
    step_scale = 1.0 / math.sqrt(PANEL)
    lane = lax.broadcasted_iota(jnp.int32, (1, LANES), 1)
    low = lane < PANEL
    sign = jnp.where(low, -1.0, 1.0).astype(jnp.float32)
    flat_cur = cur.reshape(CHUNKS * SPIN * group * local_k, LANES)
    flat_ret = ret.reshape(CHUNKS * SPIN * group * local_k, LANES)

    def swap(x):
        return pltpu.roll(x, PANEL, 1)

    def rot(x):
        return swap(x) * sign

    barrier = pltpu.get_barrier_semaphore()
    for o in range(1, n_mom):
        pl.semaphore_signal(barrier, inc=1, device_id={"mom": lax.rem(mom + o, n_mom)}, device_id_type=MESH)
    for o in range(1, n_tm):
        pl.semaphore_signal(barrier, inc=1, device_id={"tm": lax.rem(tm + o, n_tm)}, device_id_type=MESH)

    mine = pl.ds(mom * local_k, local_k)
    own_half = pl.ds(core * half, half)
    other_half = pl.ds((1 - core) * half, half)
    share_at = core * half + tm_x * share
    own_share = pl.ds(share_at, share)
    partner = {"tm": tm_x * 2 + (1 - core)}

    def remote(source, target, send, recv_sem, device):
        return pltpu.make_async_remote_copy(
            src_ref=source, dst_ref=target, send_sem=send, recv_sem=recv_sem,
            device_id=device, device_id_type=MESH)

    def forward(n, c, o):
        peer = lax.rem(mom + o, n_mom)
        return remote(cur.at[c, :, peer], recv.at[c, :, :, mine, :], fs.at[n, c, o], fr.at[n, c, o], {"mom": peer})

    def forward_own(n, c):
        return pltpu.make_async_copy(cur.at[c, :, mom], recv.at[c, :, :, mine, :], local_sem.at[n, c, 0])

    def back(n, c, o):
        peer = lax.rem(mom + o, n_mom)
        return remote(
            sig.at[c, :, :, pl.ds(peer * local_k, local_k), :], ret.at[c, :, mom],
            rs.at[n, c, o], rr.at[n, c, o], {"mom": peer})

    def back_own(n, c):
        return pltpu.make_async_copy(sig.at[c, :, :, mine, :], ret.at[c, :, mom], local_sem.at[n, c, 1])

    def pair_up(n, c):
        return remote(part.at[c, other_half], pair_buf.at[c], ps.at[n, c], pr.at[n, c], partner)

    def scatter(n, c, o):
        peer = lax.rem(tm_x + o, n_x)
        return remote(
            part.at[c, pl.ds(core * half + peer * share, share)], ring_buf.at[c, o - 1],
            ss.at[n, c, o], sr.at[n, c, o], {"tm": peer * 2 + core})

    def gather(n, c, o):
        peer = lax.rem(tm_x + o, n_x)
        return remote(
            conv.at[c, own_share], conv.at[c, own_share],
            gs.at[n, c, o], gr.at[n, c, o], {"tm": peer * 2 + core})

    def pair_down(n, c):
        return remote(conv.at[c, own_half], conv.at[c, own_half], qs.at[n, c], qr.at[n, c], partner)

    def guess_copy(o):
        return remote(guess, guess_all.at[tm], ds.at[o], dr.at[o], {"tm": lax.rem(tm + o, n_tm)})

    def guess_local():
        return pltpu.make_async_copy(guess, guess_all.at[tm], guess_own)

    def send_forward(n, c):
        for o in range(1, n_mom):
            forward(n, c, o).start()
        forward_own(n, c).start()

    def keep_stack(n, k, s, c, value):
        turned = rot(value)
        for at, piece in ((c * group, value), (PANEL + c * group, turned)):
            high, rest = split(piece)
            stk[n, 0, k, s, at:at + group, :] = high
            stk[n, 1, k, s, at:at + group, :] = rest

    def first_layout(c):
        @pl.loop(0, local_k)
        def _(k):
            for s in range(SPIN):
                at = ((c * SPIN + s) * group) * local_k + k
                flat_cur[pl.ds(at, group, stride=local_k), :] = start[k, s, c]

    def sigma(n, c):
        for o in range(1, n_mom):
            forward(n, c, o).wait_recv()
        forward_own(n, c).wait()
        if n > 0:
            for o in range(1, n_mom):
                back(n - 1, c, o).wait_send()

        @pl.loop(0, rows)
        def _(i):
            both = jnp.concatenate([recv[c, 0, i], recv[c, 1, i]], axis=1)
            sums = dot3((fwd_split[0], fwd_split[1]), split(both))
            site, mirrored = [], []
            for s in range(SPIN):
                with_cos = sums[:K, s * LANES:(s + 1) * LANES]
                turned = rot(sums[K:, s * LANES:(s + 1) * LANES])
                site.append(with_cos + turned)
                mirrored.append(with_cos - turned)
            first, second = site
            flipped = swap(second)
            pair = (first * jnp.where(low, second, flipped)
                    + rot(first) * jnp.where(low, flipped, second)) * wvec[...]
            pair_rot = rot(pair)
            tops, bottoms = [], []
            for s in range(SPIN):
                other = mirrored[1 - s]
                flipped = swap(other)
                value = pair * jnp.where(low, other, flipped) - pair_rot * jnp.where(low, flipped, other)
                tops.append(value)
                bottoms.append(-rot(value))
            stacked = jnp.concatenate(
                [jnp.concatenate(tops, axis=1), jnp.concatenate(bottoms, axis=1)], axis=0)
            result = dot3((back_split[0], back_split[1]), split(stacked))
            for s in range(SPIN):
                sig[c, s, i] = result[:, s * LANES:(s + 1) * LANES]

        for o in range(1, n_mom):
            back(n, c, o).start()
        back_own(n, c).start()

    def convolve(n, c):
        for o in range(1, n_mom):
            back(n, c, o).wait_recv()
        back_own(n, c).wait()
        if n > 0:
            pair_up(n - 1, c).wait_send()
            pair_down(n - 1, c).wait_send()
            for o in range(1, n_x):
                scatter(n - 1, c, o).wait_send()
                gather(n - 1, c, o).wait_send()

        def some(base):
            @pl.loop(0, half, unroll=2)
            def _(i):
                k = base + i
                for s in range(SPIN):
                    at = ((c * SPIN + s) * group) * local_k + k
                    value = split(flat_ret[pl.ds(at, group, stride=local_k), :])
                    part[c, k, s] = dot3(value, (stk[n, 0, k, s], stk[n, 1, k, s]), True)

        some((1 - core) * half)
        pair_up(n, c).start()
        some(core * half)

    def reduce(n, c):
        pair_up(n, c).wait_recv()

        @pl.loop(0, half)
        def _(i):
            part[c, core * half + i] = part[c, core * half + i] + pair_buf[c, i]

        for o in range(1, n_x):
            scatter(n, c, o).start()
        for o in range(1, n_x):
            scatter(n, c, o).wait_recv()

        @pl.loop(0, share)
        def _(i):
            total = part[c, share_at + i]
            for o in range(1, n_x):
                total = total + ring_buf[c, o - 1, i]
            conv[c, share_at + i] = total

        for o in range(1, n_x):
            gather(n, c, o).start()
        for o in range(1, n_x):
            gather(n, c, o).wait_recv()
        pair_down(n, c).start()

    def update(n, c):
        last = n == PASSES - 1
        if not last:
            for o in range(1, n_mom):
                forward(n, c, o).wait_send()

        def some(base):
            @pl.loop(0, half, unroll=2)
            def _(i):
                k = base + i
                for s in range(SPIN):
                    new = start[k, s, c] + step_scale * dot3(
                        split(conv[c, k, s]), (stk[n, 0, k, s], stk[n, 1, k, s]))
                    if last:
                        out[k, s, c] = new
                    else:
                        at = ((c * SPIN + s) * group) * local_k + k
                        flat_cur[pl.ds(at, group, stride=local_k), :] = new
                        keep_stack(n + 1, k, s, c, new)

        some(core * half)
        pair_down(n, c).wait_recv()
        some((1 - core) * half)

    first_layout(0)
    pl.semaphore_wait(barrier, n_mom + n_tm - 2)
    send_forward(0, 0)
    for c in range(1, CHUNKS):
        first_layout(c)
        send_forward(0, c)
    for o in range(1, n_tm):
        guess_copy(o).start()
    guess_local().start()

    fwd_split[0], fwd_split[1] = split(fwd_table[...])
    back_split[0], back_split[1] = split(back_table[...])

    @pl.loop(0, local_k)
    def _(k):
        for s in range(SPIN):
            for c in range(CHUNKS):
                keep_stack(0, k, s, c, start[k, s, c])

    for n in range(PASSES):
        for c in range(CHUNKS):
            sigma(n, c)
        for c in range(CHUNKS):
            convolve(n, c)
            reduce(n, c)
            update(n, c)
            if n < PASSES - 1:
                send_forward(n + 1, c)

    for o in range(1, n_tm):
        guess_copy(o).wait_recv()
    guess_local().wait()

    @pl.loop(0, local_k)
    def _(k):
        for s in range(SPIN):
            d = jnp.concatenate([guess_all[t, k, s] for t in range(n_tm)], axis=0)
            whole = jnp.concatenate([conv[c, k, s] for c in range(CHUNKS)], axis=0)
            stacked = jnp.concatenate([whole, rot(whole)], axis=0)
            block = d + step_scale * dot3(split(d), split(stacked))
            for c in range(CHUNKS):
                out[k, s, c] = jnp.where(
                    chosen[...] > 0.5, block[c * group:(c + 1) * group, :], out[k, s, c])

    n = PASSES - 1
    for c in range(CHUNKS):
        pair_up(n, c).wait_send()
        pair_down(n, c).wait_send()
        for o in range(1, n_x):
            scatter(n, c, o).wait_send()
            gather(n, c, o).wait_send()
        for o in range(1, n_mom):
            forward(n, c, o).wait_send()
            back(n, c, o).wait_send()
    for o in range(1, n_tm):
        guess_copy(o).wait_send()


def panel_step(n_mom, n_tm, start, guess, fwd_table, back_table, wvec, chosen):
    local_k = start.shape[0]
    group = start.shape[3]
    rows = group // n_mom
    share = local_k // n_tm
    panel = (CHUNKS, SPIN, n_mom, rows, local_k, LANES)
    sites = (CHUNKS, SPIN, rows, K, LANES)
    f32, bf16 = jnp.float32, jnp.bfloat16
    dma = pltpu.SemaphoreType.DMA
    vmem = pl.BlockSpec(memory_space=pltpu.VMEM)
    one, many_mom, many_x = (PASSES, CHUNKS), (PASSES, CHUNKS, n_mom), (PASSES, CHUNKS, n_tm // 2)
    return pl.pallas_call(
        functools.partial(step_kernel, n_mom, n_tm),
        out_shape=jax.ShapeDtypeStruct(start.shape, f32),
        in_specs=[vmem] * 6,
        out_specs=vmem,
        scratch_shapes=[
            pltpu.VMEM(panel, f32),
            pltpu.VMEM(sites, f32),
            pltpu.VMEM(sites, f32),
            pltpu.VMEM(panel, f32),
            pltpu.VMEM((2, 2 * K, K), bf16),
            pltpu.VMEM((2, K, 2 * K), bf16),
            pltpu.VMEM((PASSES, 2, local_k, SPIN, LANES, LANES), bf16),
            pltpu.VMEM((CHUNKS, local_k, SPIN, group, LANES), f32),
            pltpu.VMEM((CHUNKS, local_k, SPIN, group, LANES), f32),
            pltpu.VMEM((CHUNKS, local_k // 2, SPIN, group, LANES), f32),
            pltpu.VMEM((CHUNKS, max(n_tm // 2 - 1, 1), share, SPIN, group, LANES), f32),
            pltpu.VMEM((n_tm,) + guess.shape, f32),
            dma(one + (2,)), dma,
            dma(many_mom), dma(many_mom), dma(many_mom), dma(many_mom),
            dma(one), dma(one),
            dma(many_x), dma(many_x), dma(many_x), dma(many_x),
            dma(one), dma(one),
            dma((n_tm,)), dma((n_tm,)),
        ],
        compiler_params=pltpu.CompilerParams(
            collective_id=0, has_side_effects=True, vmem_limit_bytes=63 * 1024 * 1024),
        name="panel_step",
    )(start, guess, fwd_table, back_table, wvec, chosen)


def body(panel_start, block_guess, coupling, slab_owner, expiring, ordering):
    slab_count = lax.axis_size("tm")
    n_mom = lax.axis_size("mom")
    own_index = lax.axis_index("tm")
    cos_table, sin_table = tables(ordering)
    fwd_table = jnp.concatenate([cos_table, sin_table], axis=0)
    back_table = jnp.concatenate([cos_table.T, sin_table.T], axis=1)
    blocks = jnp.arange(slab_count, dtype=jnp.int32)
    slab_mine = jnp.sum(blocks * (slab_owner == own_index).astype(jnp.int32))
    position = (slab_mine - expiring[0]) % slab_count
    window = slab_count * PANEL
    times = position * PANEL + jnp.arange(PANEL, dtype=jnp.int32)
    weights = jnp.exp(-1.5 * (window - 1 - times).astype(jnp.float32) / window) / math.sqrt(window)
    strength = coupling[0] * coupling[0]
    wvec = (strength * jnp.concatenate([weights, weights]))[None, :]
    owner_expiring = jnp.sum(slab_owner * (blocks == expiring[0]).astype(jnp.int32))
    chosen = jnp.broadcast_to((own_index == owner_expiring).astype(jnp.float32), (1, LANES))
    local_k = panel_start.shape[0]
    start = panel_start.reshape(local_k, SPIN, CHUNKS, PANEL // CHUNKS, LANES)
    result = panel_step(n_mom, slab_count, start, block_guess, fwd_table, back_table, wvec, chosen)
    return result.reshape(panel_start.shape)


def solution(mesh):
    return jax.shard_map(
        body,
        mesh=mesh,
        in_specs=(
            P("mom", "groups", None, "tm"),
            P("mom", "groups", "tm", None),
            P("groups"),
            P("groups"),
            P("groups"),
            P(),
        ),
        out_specs=P("mom", "groups", None, "tm"),
        check_vma=False,
    )
```

```python
import functools
import math

import jax
import jax.numpy as jnp
from jax import lax
from jax.experimental import pallas as pl
from jax.experimental.pallas import tpu as pltpu
from jax.sharding import PartitionSpec as P

LSIDE = 16
K = LSIDE * LSIDE
PANEL = 64
PASSES = 2
SPIN = 2
LANES = 2 * PANEL
CHUNKS = 2
MESH = pl.DeviceIdType.MESH


def tables(ordering):
    site_index = jnp.arange(K, dtype=jnp.int32)
    site_x = site_index // LSIDE
    site_y = site_index % LSIDE
    mom_x = ordering // LSIDE
    mom_y = ordering % LSIDE
    phases = (site_x[:, None] * mom_x[None, :] + site_y[:, None] * mom_y[None, :]) % LSIDE
    angles = phases.astype(jnp.float32) * (2.0 * math.pi / LSIDE)
    return jnp.cos(angles) / LSIDE, jnp.sin(angles) / LSIDE


def split(x):
    high = x.astype(jnp.bfloat16)
    return high, (x - high.astype(jnp.float32)).astype(jnp.bfloat16)


def dot3(left, right, transposed=False):
    dims = (((1,), (1 if transposed else 0,)), ((), ()))

    def one(a, b):
        return lax.dot_general(a, b, dims, preferred_element_type=jnp.float32)

    return one(left[0], right[0]) + (one(left[0], right[1]) + one(left[1], right[0]))


def step_kernel(
    n_mom, n_tm, start, guess, fwd_table, back_table, wvec, chosen,
    out, cur, recv, sig, ret, fwd_split, back_split, stk, part, conv, pair_buf, ring_buf, guess_all,
    local_sem, guess_own, fs, fr, rs, rr, ps, pr, ss, sr, gs, gr, qs, qr, ds, dr,
):
    mom, tm = lax.axis_index("mom"), lax.axis_index("tm")
    rows, local_k = cur.shape[3], cur.shape[4]
    group = n_mom * rows
    n_x = n_tm // 2
    half = local_k // 2
    share = half // n_x
    tm_x, core = tm // 2, tm % 2
    step_scale = 1.0 / math.sqrt(PANEL)
    lane = lax.broadcasted_iota(jnp.int32, (1, LANES), 1)
    low = lane < PANEL
    sign = jnp.where(low, -1.0, 1.0).astype(jnp.float32)
    flat_cur = cur.reshape(CHUNKS * SPIN * group * local_k, LANES)
    flat_ret = ret.reshape(CHUNKS * SPIN * group * local_k, LANES)

    def swap(x):
        return pltpu.roll(x, PANEL, 1)

    def rot(x):
        return swap(x) * sign

    barrier = pltpu.get_barrier_semaphore()
    for o in range(1, n_mom):
        pl.semaphore_signal(barrier, inc=1, device_id={"mom": lax.rem(mom + o, n_mom)}, device_id_type=MESH)
    for o in range(1, n_tm):
        pl.semaphore_signal(barrier, inc=1, device_id={"tm": lax.rem(tm + o, n_tm)}, device_id_type=MESH)

    mine = pl.ds(mom * local_k, local_k)
    own_half = pl.ds(core * half, half)
    other_half = pl.ds((1 - core) * half, half)
    share_at = core * half + tm_x * share
    own_share = pl.ds(share_at, share)
    partner = {"tm": tm_x * 2 + (1 - core)}

    def remote(source, target, send, recv_sem, device):
        return pltpu.make_async_remote_copy(
            src_ref=source, dst_ref=target, send_sem=send, recv_sem=recv_sem,
            device_id=device, device_id_type=MESH)

    def forward(n, c, o):
        peer = lax.rem(mom + o, n_mom)
        return remote(cur.at[c, :, peer], recv.at[c, :, :, mine, :], fs.at[n, c, o], fr.at[n, c, o], {"mom": peer})

    def forward_own(n, c):
        return pltpu.make_async_copy(cur.at[c, :, mom], recv.at[c, :, :, mine, :], local_sem.at[n, c, 0])

    def back(n, c, o):
        peer = lax.rem(mom + o, n_mom)
        return remote(
            sig.at[c, :, :, pl.ds(peer * local_k, local_k), :], ret.at[c, :, mom],
            rs.at[n, c, o], rr.at[n, c, o], {"mom": peer})

    def back_own(n, c):
        return pltpu.make_async_copy(sig.at[c, :, :, mine, :], ret.at[c, :, mom], local_sem.at[n, c, 1])

    def pair_up(n, c):
        return remote(part.at[c, other_half], pair_buf.at[c], ps.at[n, c], pr.at[n, c], partner)

    def scatter(n, c, o):
        peer = lax.rem(tm_x + o, n_x)
        return remote(
            part.at[c, pl.ds(core * half + peer * share, share)], ring_buf.at[c, o - 1],
            ss.at[n, c, o], sr.at[n, c, o], {"tm": peer * 2 + core})

    def gather(n, c, o):
        peer = lax.rem(tm_x + o, n_x)
        return remote(
            conv.at[c, own_share], conv.at[c, own_share],
            gs.at[n, c, o], gr.at[n, c, o], {"tm": peer * 2 + core})

    def pair_down(n, c):
        return remote(conv.at[c, own_half], conv.at[c, own_half], qs.at[n, c], qr.at[n, c], partner)

    def guess_copy(o):
        return remote(guess, guess_all.at[tm], ds.at[o], dr.at[o], {"tm": lax.rem(tm + o, n_tm)})

    def guess_local():
        return pltpu.make_async_copy(guess, guess_all.at[tm], guess_own)

    def send_forward(n, c):
        for o in range(1, n_mom):
            forward(n, c, o).start()
        forward_own(n, c).start()

    def keep_stack(n, k, s, c, value):
        turned = rot(value)
        for at, piece in ((c * group, value), (PANEL + c * group, turned)):
            high, rest = split(piece)
            stk[n, 0, k, s, at:at + group, :] = high
            stk[n, 1, k, s, at:at + group, :] = rest

    def first_layout(c):
        @pl.loop(0, local_k)
        def _(k):
            for s in range(SPIN):
                at = ((c * SPIN + s) * group) * local_k + k
                flat_cur[pl.ds(at, group, stride=local_k), :] = start[k, s, c]

    def sigma(n, c):
        for o in range(1, n_mom):
            forward(n, c, o).wait_recv()
        forward_own(n, c).wait()
        if n > 0:
            for o in range(1, n_mom):
                back(n - 1, c, o).wait_send()

        @pl.loop(0, rows)
        def _(i):
            both = jnp.concatenate([recv[c, 0, i], recv[c, 1, i]], axis=1)
            sums = dot3((fwd_split[0], fwd_split[1]), split(both))
            site, mirrored = [], []
            for s in range(SPIN):
                with_cos = sums[:K, s * LANES:(s + 1) * LANES]
                turned = rot(sums[K:, s * LANES:(s + 1) * LANES])
                site.append(with_cos + turned)
                mirrored.append(with_cos - turned)
            first, second = site
            flipped = swap(second)
            pair = (first * jnp.where(low, second, flipped)
                    + rot(first) * jnp.where(low, flipped, second)) * wvec[...]
            pair_rot = rot(pair)
            tops, bottoms = [], []
            for s in range(SPIN):
                other = mirrored[1 - s]
                flipped = swap(other)
                value = pair * jnp.where(low, other, flipped) - pair_rot * jnp.where(low, flipped, other)
                tops.append(value)
                bottoms.append(-rot(value))
            stacked = jnp.concatenate(
                [jnp.concatenate(tops, axis=1), jnp.concatenate(bottoms, axis=1)], axis=0)
            result = dot3((back_split[0], back_split[1]), split(stacked))
            for s in range(SPIN):
                sig[c, s, i] = result[:, s * LANES:(s + 1) * LANES]

        for o in range(1, n_mom):
            back(n, c, o).start()
        back_own(n, c).start()

    def convolve(n, c):
        for o in range(1, n_mom):
            back(n, c, o).wait_recv()
        back_own(n, c).wait()
        if n > 0:
            pair_up(n - 1, c).wait_send()
            pair_down(n - 1, c).wait_send()
            for o in range(1, n_x):
                scatter(n - 1, c, o).wait_send()
                gather(n - 1, c, o).wait_send()

        def some(base):
            @pl.loop(0, half, unroll=8)
            def _(i):
                k = base + i
                for s in range(SPIN):
                    at = ((c * SPIN + s) * group) * local_k + k
                    value = split(flat_ret[pl.ds(at, group, stride=local_k), :])
                    part[c, k, s] = dot3(value, (stk[n, 0, k, s], stk[n, 1, k, s]), True)

        some((1 - core) * half)
        pair_up(n, c).start()
        some(core * half)

    def reduce(n, c):
        pair_up(n, c).wait_recv()

        @pl.loop(0, half)
        def _(i):
            part[c, core * half + i] = part[c, core * half + i] + pair_buf[c, i]

        for o in range(1, n_x):
            scatter(n, c, o).start()
        for o in range(1, n_x):
            scatter(n, c, o).wait_recv()

        @pl.loop(0, share)
        def _(i):
            total = part[c, share_at + i]
            for o in range(1, n_x):
                total = total + ring_buf[c, o - 1, i]
            conv[c, share_at + i] = total

        for o in range(1, n_x):
            gather(n, c, o).start()
        for o in range(1, n_x):
            gather(n, c, o).wait_recv()
        pair_down(n, c).start()

    def update(n, c):
        for o in range(1, n_mom):
            forward(n, c, o).wait_send()

        def some(base):
            @pl.loop(0, half, unroll=8)
            def _(i):
                k = base + i
                for s in range(SPIN):
                    new = start[k, s, c] + step_scale * dot3(
                        split(conv[c, k, s]), (stk[n, 0, k, s], stk[n, 1, k, s]))
                    at = ((c * SPIN + s) * group) * local_k + k
                    flat_cur[pl.ds(at, group, stride=local_k), :] = new
                    keep_stack(n + 1, k, s, c, new)

        some(core * half)
        pair_down(n, c).wait_recv()
        some((1 - core) * half)

    def finish(n):
        is_block = chosen[...] > 0.5

        def some(base):
            @pl.loop(0, half, unroll=4)
            def _(i):
                k = base + i
                for s in range(SPIN):
                    whole = jnp.concatenate([conv[c, k, s] for c in range(CHUNKS)], axis=0)
                    d = jnp.concatenate([guess_all[t, k, s] for t in range(n_tm)], axis=0)
                    first = jnp.concatenate([start[k, s, c] for c in range(CHUNKS)], axis=0)
                    panel = stk[n, 0, k, s].astype(jnp.float32) + stk[n, 1, k, s].astype(jnp.float32)
                    right = jnp.where(is_block, jnp.concatenate([whole, rot(whole)], axis=0), panel)
                    left = jnp.where(is_block, d, whole)
                    new = jnp.where(is_block, d, first) + step_scale * dot3(split(left), split(right))
                    for c in range(CHUNKS):
                        out[k, s, c] = new[c * group:(c + 1) * group, :]

        for c in range(CHUNKS - 1):
            pair_down(n, c).wait_recv()
        some(core * half)
        pair_down(n, CHUNKS - 1).wait_recv()
        some((1 - core) * half)

    first_layout(0)
    pl.semaphore_wait(barrier, n_mom + n_tm - 2)
    send_forward(0, 0)
    for c in range(1, CHUNKS):
        first_layout(c)
        send_forward(0, c)
    for o in range(1, n_tm):
        guess_copy(o).start()
    guess_local().start()

    fwd_split[0], fwd_split[1] = split(fwd_table[...])
    back_split[0], back_split[1] = split(back_table[...])

    @pl.loop(0, local_k, unroll=4)
    def _(k):
        for s in range(SPIN):
            for c in range(CHUNKS):
                keep_stack(0, k, s, c, start[k, s, c])

    for n in range(PASSES):
        for c in range(CHUNKS):
            sigma(n, c)
        for c in range(CHUNKS):
            convolve(n, c)
            reduce(n, c)
            if n < PASSES - 1:
                update(n, c)
                send_forward(n + 1, c)

    for o in range(1, n_tm):
        guess_copy(o).wait_recv()
    guess_local().wait()
    finish(PASSES - 1)

    n = PASSES - 1
    for c in range(CHUNKS):
        pair_up(n, c).wait_send()
        pair_down(n, c).wait_send()
        for o in range(1, n_x):
            scatter(n, c, o).wait_send()
            gather(n, c, o).wait_send()
        for o in range(1, n_mom):
            forward(n, c, o).wait_send()
            back(n, c, o).wait_send()
    for o in range(1, n_tm):
        guess_copy(o).wait_send()


def panel_step(n_mom, n_tm, start, guess, fwd_table, back_table, wvec, chosen):
    local_k = start.shape[0]
    group = start.shape[3]
    rows = group // n_mom
    share = local_k // n_tm
    panel = (CHUNKS, SPIN, n_mom, rows, local_k, LANES)
    sites = (CHUNKS, SPIN, rows, K, LANES)
    f32, bf16 = jnp.float32, jnp.bfloat16
    dma = pltpu.SemaphoreType.DMA
    vmem = pl.BlockSpec(memory_space=pltpu.VMEM)
    one, many_mom, many_x = (PASSES, CHUNKS), (PASSES, CHUNKS, n_mom), (PASSES, CHUNKS, n_tm // 2)
    return pl.pallas_call(
        functools.partial(step_kernel, n_mom, n_tm),
        out_shape=jax.ShapeDtypeStruct(start.shape, f32),
        in_specs=[vmem] * 6,
        out_specs=vmem,
        scratch_shapes=[
            pltpu.VMEM(panel, f32),
            pltpu.VMEM(sites, f32),
            pltpu.VMEM(sites, f32),
            pltpu.VMEM(panel, f32),
            pltpu.VMEM((2, 2 * K, K), bf16),
            pltpu.VMEM((2, K, 2 * K), bf16),
            pltpu.VMEM((PASSES, 2, local_k, SPIN, LANES, LANES), bf16),
            pltpu.VMEM((CHUNKS, local_k, SPIN, group, LANES), f32),
            pltpu.VMEM((CHUNKS, local_k, SPIN, group, LANES), f32),
            pltpu.VMEM((CHUNKS, local_k // 2, SPIN, group, LANES), f32),
            pltpu.VMEM((CHUNKS, max(n_tm // 2 - 1, 1), share, SPIN, group, LANES), f32),
            pltpu.VMEM((n_tm,) + guess.shape, f32),
            dma(one + (2,)), dma,
            dma(many_mom), dma(many_mom), dma(many_mom), dma(many_mom),
            dma(one), dma(one),
            dma(many_x), dma(many_x), dma(many_x), dma(many_x),
            dma(one), dma(one),
            dma((n_tm,)), dma((n_tm,)),
        ],
        compiler_params=pltpu.CompilerParams(
            collective_id=0, has_side_effects=True, vmem_limit_bytes=63 * 1024 * 1024),
        name="panel_step",
    )(start, guess, fwd_table, back_table, wvec, chosen)


def body(panel_start, block_guess, coupling, slab_owner, expiring, ordering):
    slab_count = lax.axis_size("tm")
    n_mom = lax.axis_size("mom")
    own_index = lax.axis_index("tm")
    cos_table, sin_table = tables(ordering)
    fwd_table = jnp.concatenate([cos_table, sin_table], axis=0)
    back_table = jnp.concatenate([cos_table.T, sin_table.T], axis=1)
    blocks = jnp.arange(slab_count, dtype=jnp.int32)
    slab_mine = jnp.sum(blocks * (slab_owner == own_index).astype(jnp.int32))
    position = (slab_mine - expiring[0]) % slab_count
    window = slab_count * PANEL
    times = position * PANEL + jnp.arange(PANEL, dtype=jnp.int32)
    weights = jnp.exp(-1.5 * (window - 1 - times).astype(jnp.float32) / window) / math.sqrt(window)
    strength = coupling[0] * coupling[0]
    wvec = (strength * jnp.concatenate([weights, weights]))[None, :]
    owner_expiring = jnp.sum(slab_owner * (blocks == expiring[0]).astype(jnp.int32))
    chosen = jnp.broadcast_to((own_index == owner_expiring).astype(jnp.float32), (1, LANES))
    local_k = panel_start.shape[0]
    start = panel_start.reshape(local_k, SPIN, CHUNKS, PANEL // CHUNKS, LANES)
    result = panel_step(n_mom, slab_count, start, block_guess, fwd_table, back_table, wvec, chosen)
    return result.reshape(panel_start.shape)


def solution(mesh):
    return jax.shard_map(
        body,
        mesh=mesh,
        in_specs=(
            P("mom", "groups", None, "tm"),
            P("mom", "groups", "tm", None),
            P("groups"),
            P("groups"),
            P("groups"),
            P(),
        ),
        out_specs=P("mom", "groups", None, "tm"),
        check_vma=False,
    )
```

```python
import functools
import math

import jax
import jax.numpy as jnp
from jax import lax
from jax.experimental import pallas as pl
from jax.experimental.pallas import tpu as pltpu
from jax.sharding import PartitionSpec as P

LSIDE = 16
K = LSIDE * LSIDE
PANEL = 64
PASSES = 2
SPIN = 2
LANES = 2 * PANEL
CHUNKS = 2
MESH = pl.DeviceIdType.MESH


def tables(ordering):
    bits = LSIDE.bit_length() - 1
    site = lax.broadcasted_iota(jnp.int32, (K, K), 0)
    phases = ((site >> bits) * (ordering >> bits) + (site & (LSIDE - 1)) * (ordering & (LSIDE - 1))) & (LSIDE - 1)
    angles = phases.astype(jnp.float32) * (2.0 * math.pi / LSIDE)
    return jnp.cos(angles) / LSIDE, jnp.sin(angles) / LSIDE


def split(x):
    high = x.astype(jnp.bfloat16)
    return high, (x - high.astype(jnp.float32)).astype(jnp.bfloat16)


def dot3(left, right, transposed=False):
    dims = (((1,), (1 if transposed else 0,)), ((), ()))

    def one(a, b):
        return lax.dot_general(a, b, dims, preferred_element_type=jnp.float32)

    return one(left[0], right[0]) + (one(left[0], right[1]) + one(left[1], right[0]))


def step_kernel(
    n_mom, n_tm, start, guess, ordering, wvec, chosen,
    out, cur, recv, sig, ret, fwd_split, back_split, stk, part, conv, pair_buf, ring_buf, guess_all,
    local_sem, guess_own, fs, fr, rs, rr, ps, pr, ss, sr, gs, gr, qs, qr, ds, dr,
):
    mom, tm = lax.axis_index("mom"), lax.axis_index("tm")
    rows, local_k = cur.shape[3], cur.shape[4]
    group = n_mom * rows
    n_x = n_tm // 2
    half = local_k // 2
    share = half // n_x
    tm_x, core = tm // 2, tm % 2
    step_scale = 1.0 / math.sqrt(PANEL)
    lane = lax.broadcasted_iota(jnp.int32, (1, LANES), 1)
    low = lane < PANEL
    sign = jnp.where(low, -1.0, 1.0).astype(jnp.float32)
    flat_cur = cur.reshape(CHUNKS * SPIN * group * local_k, LANES)
    flat_ret = ret.reshape(CHUNKS * SPIN * group * local_k, LANES)

    def swap(x):
        return pltpu.roll(x, PANEL, 1)

    def rot(x):
        return swap(x) * sign

    barrier = pltpu.get_barrier_semaphore()
    for o in range(1, n_mom):
        pl.semaphore_signal(barrier, inc=1, device_id={"mom": lax.rem(mom + o, n_mom)}, device_id_type=MESH)
    for o in range(1, n_tm):
        pl.semaphore_signal(barrier, inc=1, device_id={"tm": lax.rem(tm + o, n_tm)}, device_id_type=MESH)

    mine = pl.ds(mom * local_k, local_k)
    other_half = pl.ds((1 - core) * half, half)
    share_at = core * half + tm_x * share
    own_share = pl.ds(share_at, share)
    partner = {"tm": tm_x * 2 + (1 - core)}

    def remote(source, target, send, recv_sem, device):
        return pltpu.make_async_remote_copy(
            src_ref=source, dst_ref=target, send_sem=send, recv_sem=recv_sem,
            device_id=device, device_id_type=MESH)

    def forward(n, c, o):
        peer = lax.rem(mom + o, n_mom)
        return remote(cur.at[c, :, peer], recv.at[c, :, :, mine, :], fs.at[n, c, o], fr.at[n, c, o], {"mom": peer})

    def forward_own(n, c):
        return pltpu.make_async_copy(cur.at[c, :, mom], recv.at[c, :, :, mine, :], local_sem.at[n, c, 0])

    def back(n, c, o):
        peer = lax.rem(mom + o, n_mom)
        return remote(
            sig.at[c, :, :, pl.ds(peer * local_k, local_k), :], ret.at[c, :, mom],
            rs.at[n, c, o], rr.at[n, c, o], {"mom": peer})

    def back_own(n, c):
        return pltpu.make_async_copy(sig.at[c, :, :, mine, :], ret.at[c, :, mom], local_sem.at[n, c, 1])

    def pair_up(n, c):
        return remote(part.at[c, other_half], pair_buf.at[c], ps.at[n, c], pr.at[n, c], partner)

    def scatter(n, c, o):
        peer = lax.rem(tm_x + o, n_x)
        return remote(
            part.at[c, pl.ds(core * half + peer * share, share)], ring_buf.at[c, o - 1],
            ss.at[n, c, o], sr.at[n, c, o], {"tm": peer * 2 + core})

    def gather(n, c, o):
        peer = lax.rem(tm_x + o, n_x)
        return remote(
            conv.at[c, own_share], conv.at[c, own_share],
            gs.at[n, c, o], gr.at[n, c, o], {"tm": peer * 2 + core})

    def pair_down(n, c, o):
        held = pl.ds(core * half + lax.rem(tm_x + n_x - o, n_x) * share, share)
        return remote(conv.at[c, held], conv.at[c, held], qs.at[n, c, o], qr.at[n, c, o], partner)

    def pair_down_recv(n, c):
        for o in range(n_x):
            pair_down(n, c, o).wait_recv()

    def guess_copy(o):
        return remote(guess, guess_all.at[tm], ds.at[o], dr.at[o], {"tm": lax.rem(tm + o, n_tm)})

    def guess_local():
        return pltpu.make_async_copy(guess, guess_all.at[tm], guess_own)

    def send_forward(n, c):
        for o in range(1, n_mom):
            forward(n, c, o).start()
        forward_own(n, c).start()

    def keep_stack(n, k, s, c, value):
        turned = rot(value)
        for at, piece in ((c * group, value), (PANEL + c * group, turned)):
            high, rest = split(piece)
            stk[n, 0, k, s, at:at + group, :] = high
            stk[n, 1, k, s, at:at + group, :] = rest

    def first_layout(c):
        @pl.loop(0, local_k)
        def _(k):
            for s in range(SPIN):
                at = ((c * SPIN + s) * group) * local_k + k
                flat_cur[pl.ds(at, group, stride=local_k), :] = start[k, s, c]

    def sigma(n, c):
        for o in range(1, n_mom):
            forward(n, c, o).wait_recv()
        forward_own(n, c).wait()
        if n > 0:
            for o in range(1, n_mom):
                back(n - 1, c, o).wait_send()

        @pl.loop(0, rows)
        def _(i):
            both = jnp.concatenate([recv[c, 0, i], recv[c, 1, i]], axis=1)
            sums = dot3((fwd_split[0], fwd_split[1]), split(both))
            site, mirrored = [], []
            for s in range(SPIN):
                with_cos = sums[:K, s * LANES:(s + 1) * LANES]
                turned = rot(sums[K:, s * LANES:(s + 1) * LANES])
                site.append(with_cos + turned)
                mirrored.append(with_cos - turned)
            first, second = site
            flipped = swap(second)
            pair = (first * jnp.where(low, second, flipped)
                    + rot(first) * jnp.where(low, flipped, second)) * wvec[...]
            pair_rot = rot(pair)
            tops, bottoms = [], []
            for s in range(SPIN):
                other = mirrored[1 - s]
                flipped = swap(other)
                value = pair * jnp.where(low, other, flipped) - pair_rot * jnp.where(low, flipped, other)
                tops.append(value)
                bottoms.append(-rot(value))
            stacked = jnp.concatenate(
                [jnp.concatenate(tops, axis=1), jnp.concatenate(bottoms, axis=1)], axis=0)
            result = dot3((back_split[0], back_split[1]), split(stacked))
            for s in range(SPIN):
                sig[c, s, i] = result[:, s * LANES:(s + 1) * LANES]

        for o in range(1, n_mom):
            back(n, c, o).start()
        back_own(n, c).start()

    def convolve(n, c):
        for o in range(1, n_mom):
            back(n, c, o).wait_recv()
        back_own(n, c).wait()
        if n > 0:
            pair_up(n - 1, c).wait_send()
            for o in range(n_x):
                pair_down(n - 1, c, o).wait_send()
            for o in range(1, n_x):
                scatter(n - 1, c, o).wait_send()
                gather(n - 1, c, o).wait_send()

        def some(base):
            @pl.loop(0, half, unroll=8)
            def _(i):
                k = base + i
                for s in range(SPIN):
                    at = ((c * SPIN + s) * group) * local_k + k
                    value = split(flat_ret[pl.ds(at, group, stride=local_k), :])
                    part[c, k, s] = dot3(value, (stk[n, 0, k, s], stk[n, 1, k, s]), True)

        some((1 - core) * half)
        pair_up(n, c).start()
        some(core * half)

    def reduce(n, c):
        pair_up(n, c).wait_recv()

        @pl.loop(0, half)
        def _(i):
            part[c, core * half + i] = part[c, core * half + i] + pair_buf[c, i]

        for o in range(1, n_x):
            scatter(n, c, o).start()
        for o in range(1, n_x):
            scatter(n, c, o).wait_recv()

        @pl.loop(0, share)
        def _(i):
            total = part[c, share_at + i]
            for o in range(1, n_x):
                total = total + ring_buf[c, o - 1, i]
            conv[c, share_at + i] = total

        for o in range(1, n_x):
            gather(n, c, o).start()
        pair_down(n, c, 0).start()
        for o in range(1, n_x):
            gather(n, c, o).wait_recv()
            pair_down(n, c, o).start()

    def update(n, c):
        for o in range(1, n_mom):
            forward(n, c, o).wait_send()

        def some(base):
            @pl.loop(0, half, unroll=8)
            def _(i):
                k = base + i
                for s in range(SPIN):
                    new = start[k, s, c] + step_scale * dot3(
                        split(conv[c, k, s]), (stk[n, 0, k, s], stk[n, 1, k, s]))
                    at = ((c * SPIN + s) * group) * local_k + k
                    flat_cur[pl.ds(at, group, stride=local_k), :] = new
                    keep_stack(n + 1, k, s, c, new)

        some(core * half)
        pair_down_recv(n, c)
        some((1 - core) * half)

    def finish(n):
        is_block = chosen[...] > 0.5

        def some(base):
            @pl.loop(0, half, unroll=4)
            def _(i):
                k = base + i
                for s in range(SPIN):
                    whole = jnp.concatenate([conv[c, k, s] for c in range(CHUNKS)], axis=0)
                    d = jnp.concatenate([guess_all[t, k, s] for t in range(n_tm)], axis=0)
                    first = jnp.concatenate([start[k, s, c] for c in range(CHUNKS)], axis=0)
                    panel = stk[n, 0, k, s].astype(jnp.float32) + stk[n, 1, k, s].astype(jnp.float32)
                    right = jnp.where(is_block, jnp.concatenate([whole, rot(whole)], axis=0), panel)
                    left = jnp.where(is_block, d, whole)
                    new = jnp.where(is_block, d, first) + step_scale * dot3(split(left), split(right))
                    for c in range(CHUNKS):
                        out[k, s, c] = new[c * group:(c + 1) * group, :]

        for c in range(CHUNKS - 1):
            pair_down_recv(n, c)
        some(core * half)
        pair_down_recv(n, CHUNKS - 1)
        some((1 - core) * half)

    first_layout(0)
    pl.semaphore_wait(barrier, n_mom + n_tm - 2)
    send_forward(0, 0)
    for c in range(1, CHUNKS):
        first_layout(c)
        send_forward(0, c)
    for o in range(1, n_tm):
        guess_copy(o).start()
    guess_local().start()

    for at, table in enumerate(tables(ordering[...])):
        fwd_split[0, at * K:(at + 1) * K, :], fwd_split[1, at * K:(at + 1) * K, :] = split(table)
        turned = split(table.T)
        back_split[0, :, at * K:(at + 1) * K], back_split[1, :, at * K:(at + 1) * K] = turned

    @pl.loop(0, local_k, unroll=4)
    def _(k):
        for s in range(SPIN):
            for c in range(CHUNKS):
                keep_stack(0, k, s, c, start[k, s, c])

    for n in range(PASSES):
        for c in range(CHUNKS):
            sigma(n, c)
        for c in range(CHUNKS):
            convolve(n, c)
            reduce(n, c)
            if n < PASSES - 1:
                update(n, c)
                send_forward(n + 1, c)

    for o in range(1, n_tm):
        guess_copy(o).wait_recv()
    guess_local().wait()
    finish(PASSES - 1)

    n = PASSES - 1
    for c in range(CHUNKS):
        pair_up(n, c).wait_send()
        for o in range(n_x):
            pair_down(n, c, o).wait_send()
        for o in range(1, n_x):
            scatter(n, c, o).wait_send()
            gather(n, c, o).wait_send()
        for o in range(1, n_mom):
            forward(n, c, o).wait_send()
            back(n, c, o).wait_send()
    for o in range(1, n_tm):
        guess_copy(o).wait_send()


def panel_step(n_mom, n_tm, start, guess, ordering, wvec, chosen):
    local_k = start.shape[0]
    group = start.shape[3]
    rows = group // n_mom
    share = local_k // n_tm
    panel = (CHUNKS, SPIN, n_mom, rows, local_k, LANES)
    sites = (CHUNKS, SPIN, rows, K, LANES)
    f32, bf16 = jnp.float32, jnp.bfloat16
    dma = pltpu.SemaphoreType.DMA
    vmem = pl.BlockSpec(memory_space=pltpu.VMEM)
    one, many_mom, many_x = (PASSES, CHUNKS), (PASSES, CHUNKS, n_mom), (PASSES, CHUNKS, n_tm // 2)
    return pl.pallas_call(
        functools.partial(step_kernel, n_mom, n_tm),
        out_shape=jax.ShapeDtypeStruct(start.shape, f32),
        in_specs=[vmem] * 5,
        out_specs=vmem,
        scratch_shapes=[
            pltpu.VMEM(panel, f32),
            pltpu.VMEM(sites, f32),
            pltpu.VMEM(sites, f32),
            pltpu.VMEM(panel, f32),
            pltpu.VMEM((2, 2 * K, K), bf16),
            pltpu.VMEM((2, K, 2 * K), bf16),
            pltpu.VMEM((PASSES, 2, local_k, SPIN, LANES, LANES), bf16),
            pltpu.VMEM((CHUNKS, local_k, SPIN, group, LANES), f32),
            pltpu.VMEM((CHUNKS, local_k, SPIN, group, LANES), f32),
            pltpu.VMEM((CHUNKS, local_k // 2, SPIN, group, LANES), f32),
            pltpu.VMEM((CHUNKS, max(n_tm // 2 - 1, 1), share, SPIN, group, LANES), f32),
            pltpu.VMEM((n_tm,) + guess.shape, f32),
            dma(one + (2,)), dma,
            dma(many_mom), dma(many_mom), dma(many_mom), dma(many_mom),
            dma(one), dma(one),
            dma(many_x), dma(many_x), dma(many_x), dma(many_x),
            dma(many_x), dma(many_x),
            dma((n_tm,)), dma((n_tm,)),
        ],
        compiler_params=pltpu.CompilerParams(
            collective_id=0, has_side_effects=True, vmem_limit_bytes=63 * 1024 * 1024),
        name="panel_step",
    )(start, guess, ordering, wvec, chosen)


def body(panel_start, block_guess, coupling, slab_owner, expiring, ordering):
    slab_count = lax.axis_size("tm")
    n_mom = lax.axis_size("mom")
    own_index = lax.axis_index("tm")
    blocks = jnp.arange(slab_count, dtype=jnp.int32)
    slab_mine = jnp.sum(blocks * (slab_owner == own_index).astype(jnp.int32))
    position = (slab_mine - expiring[0]) % slab_count
    window = slab_count * PANEL
    times = position * PANEL + jnp.arange(PANEL, dtype=jnp.int32)
    weights = jnp.exp(-1.5 * (window - 1 - times).astype(jnp.float32) / window) / math.sqrt(window)
    strength = coupling[0] * coupling[0]
    wvec = (strength * jnp.concatenate([weights, weights]))[None, :]
    owner_expiring = jnp.sum(slab_owner * (blocks == expiring[0]).astype(jnp.int32))
    chosen = jnp.broadcast_to((own_index == owner_expiring).astype(jnp.float32), (1, LANES))
    local_k = panel_start.shape[0]
    start = panel_start.reshape(local_k, SPIN, CHUNKS, PANEL // CHUNKS, LANES)
    result = panel_step(n_mom, slab_count, start, block_guess, ordering[None, :], wvec, chosen)
    return result.reshape(panel_start.shape)


def solution(mesh):
    return jax.shard_map(
        body,
        mesh=mesh,
        in_specs=(
            P("mom", "groups", None, "tm"),
            P("mom", "groups", "tm", None),
            P("groups"),
            P("groups"),
            P("groups"),
            P(),
        ),
        out_specs=P("mom", "groups", None, "tm"),
        check_vma=False,
    )
```
